32 devices in a mesh: tm: 4 (over y, x), space: 2 (over core), ens: 4 (over z).
Axes of the slice: x: 2, y: 2, z: 4, core: 2. Of those that a mesh axis runs over, the one named last changes fastest.
Arguments:
- initial_state: float32 [4, 4, 32, 512], P('ens', None, 'space'), may hold values from -6 to 6
- forcing: float32 [2, 32, 512], P(None, 'space'), may hold values from -6 to 6
- w_down: bfloat16 [128, 16], replicated, may hold values from -1.5 to 1.5
- depth_kernel: float32 [2, 128, 9], replicated, may hold values from -2 to 2
- w_point: bfloat16 [2, 128, 128], replicated, may hold values from -0.5 to 0.5
- w_up: bfloat16 [16, 128], replicated, may hold values from -0.25 to 0.25
Outputs:
- slice_ends: float32 [4, 4, 4, 32, 512], P('ens', 'tm', None, 'space')
- ensemble_mean: float32 [4, 4, 32, 512], P('tm', None, 'space')
The draws below stay inside these ranges and needn't reach their ends.
All inputs are finite; a program needn't handle non-finite values.
Results may differ from the reference program's by a relative error of at most 0.0084.
Values may be sent and summed in bfloat16 or wider, within the bound.
A program may use at most 64 MiB of HBM per device.

```python
import jax
import jax.numpy as jnp

FIELDS = 4
CH = 128
LAYERS = 2
ITERS = 2
FINE = 4
COLS = 512
NROWS = 32
SLICES = 4
MEMBERS = 4


def steps_of(own_key, shape, shards, least, top_value):
    loudness = 1.0
    for dim, shards_of in shards:
        steps = jax.random.uniform(jax.random.fold_in(jax.random.fold_in(own_key, 6), dim), (shards_of,), jnp.float32, least / len(shards), top_value / len(shards))
        loudness = loudness * jnp.repeat(jnp.exp(steps), shape[dim] // shards_of).reshape((-1,) + (1,) * (len(shape) - 1 - dim))
    return loudness


def normal_values(rng, dims, scale, reach, split=(), held_as=jnp.bfloat16):
    gain = steps_of(rng, dims, split, -0.22, 0.18) if split else 1.0
    array = jax.random.normal(rng, dims, jnp.float32) * scale * gain
    return jnp.minimum(jnp.maximum(array, -reach), reach).astype(held_as)


def setup_inputs(seed: int = 0) -> dict:
    splits = jax.random.split(jax.random.key(seed), 7)
    initial_state = normal_values(splits[0], (MEMBERS, FIELDS, NROWS, COLS), 1.0, 6.0, ((0, 4), (2, 2)), jnp.float32)
    forcing = normal_values(splits[1], (2, NROWS, COLS), 1.0, 6.0, ((1, 2),), jnp.float32)
    w_down = normal_values(splits[2], (CH, 4 * FIELDS), (4 * FIELDS) ** -0.5, 1.5)
    depth_kernel = normal_values(splits[3], (LAYERS, CH, 9), 9 ** -0.5, 2.0, (), jnp.float32)
    w_point = normal_values(splits[4], (LAYERS, CH, CH), CH ** -0.5, 0.5)
    w_up = normal_values(splits[5], (4 * FIELDS, CH), (4 * CH) ** -0.5, 0.25)
    return dict(initial_state=initial_state, forcing=forcing, w_down=w_down, depth_kernel=depth_kernel, w_point=w_point, w_up=w_up)


TIME_STEP = 0.05
VISCOSITY = 0.5
WAVE_SQ = 1.0
DIFFUSIVITY = 0.3


def advance(center, northern, southern, eastern, western, forcing):
    across = (eastern - western) * 0.5
    downward = (southern - northern) * 0.5
    laplace = northern + southern + eastern + western - 4.0 * center
    carried = center[0] * across + center[1] * downward
    rate_u = -carried[0] - across[2] + VISCOSITY * laplace[0] + forcing[0]
    rate_v = -carried[1] - downward[2] + VISCOSITY * laplace[1] + forcing[1]
    rate_p = -WAVE_SQ * (across[0] + downward[1]) + VISCOSITY * laplace[2]
    rate_s = -carried[3] + DIFFUSIVITY * laplace[3]
    return center + TIME_STEP * jnp.stack([rate_u, rate_v, rate_p, rate_s])


def fine_ref(state_in, forcing):
    for substep in range(FINE):
        state_in = advance(state_in, jnp.roll(state_in, 1, axis=1), jnp.roll(state_in, -1, axis=1),
                           jnp.roll(state_in, -1, axis=2), jnp.roll(state_in, 1, axis=2), forcing)
    return state_in


def to_patches(grid):
    fields, height, columns = grid.shape
    grouped = grid.reshape(fields, height // 2, 2, columns // 2, 2).transpose(0, 2, 4, 1, 3)
    return grouped.reshape(fields * 4, height // 2, columns // 2)


def from_patches(coarse_out, fields):
    height, columns = coarse_out.shape[1], coarse_out.shape[2]
    grouped = coarse_out.reshape(fields, 2, 2, height, columns).transpose(0, 3, 1, 4, 2)
    return grouped.reshape(fields, height * 2, columns * 2)


def depthwise_ref(hidden, kernel):
    summed = jnp.zeros(hidden.shape, jnp.float32)
    for offset_row in (-1, 0, 1):
        band = jnp.roll(hidden, -offset_row, axis=1).astype(jnp.float32)
        for offset_col in (-1, 0, 1):
            tap = kernel[:, (offset_row + 1) * 3 + offset_col + 1].astype(jnp.float32)
            summed = summed + tap[:, None, None] * jnp.roll(band, -offset_col, axis=2)
    return summed


def coarse_ref(state_in, w_down, depth_kernel, w_point, w_up):
    patches = to_patches(state_in.astype(jnp.bfloat16))
    hidden = jnp.einsum("cq,qrw->crw", w_down.astype(jnp.float32), patches.astype(jnp.float32)).astype(jnp.bfloat16)
    for depth_level in range(LAYERS):
        filtered = depthwise_ref(hidden, depth_kernel[depth_level]).astype(jnp.bfloat16)
        lifted = jnp.einsum("oc,crw->orw", w_point[depth_level].astype(jnp.float32), filtered.astype(jnp.float32))
        hidden = (hidden.astype(jnp.float32) + jax.nn.gelu(lifted)).astype(jnp.bfloat16)
    output = jnp.einsum("qc,crw->qrw", w_up.astype(jnp.float32), hidden.astype(jnp.float32))
    return state_in + from_patches(output, state_in.shape[0])


def reference(initial_state, forcing, w_down, depth_kernel, w_point, w_up):
    def coarse(state_in):
        return coarse_ref(state_in, w_down, depth_kernel, w_point, w_up)

    every_member = []
    for member in range(MEMBERS):
        anchor = initial_state[member]
        starts = [anchor]
        coarse_old = []
        for slice_index in range(SLICES - 1):
            predicted = coarse(starts[-1])
            coarse_old.append(predicted)
            starts.append(predicted)
        coarse_old.append(coarse(starts[-1]))
        endings = []
        for rounds in range(ITERS):
            corrections = [fine_ref(starts[slice_index], forcing) - coarse_old[slice_index] for slice_index in range(SLICES)]
            refreshed = [anchor]
            coarse_new = []
            for slice_index in range(SLICES - 1):
                predicted = coarse(refreshed[-1])
                coarse_new.append(predicted)
                refreshed.append(predicted + corrections[slice_index])
            coarse_new.append(coarse(refreshed[-1]))
            endings = [coarse_new[slice_index] + corrections[slice_index] for slice_index in range(SLICES)]
            starts, coarse_old = refreshed, coarse_new
        every_member.append(jnp.stack(endings))
    slice_ends = jnp.stack(every_member)
    ensemble_mean = jnp.sum(slice_ends, axis=0) / MEMBERS
    return slice_ends, ensemble_mean
```

```python
import jax
import jax.numpy as jnp
from jax import lax
from jax.experimental import pallas as pl
from jax.experimental.pallas import tpu as pltpu
from jax.sharding import PartitionSpec as P

TIME_STEP = 0.05
VISCOSITY = 0.5
DIFFUSIVITY = 0.3
FINE = 4
MESH = pl.DeviceIdType.MESH
F32 = jnp.float32
BF16 = jnp.bfloat16


def swap_order(p):
    return p + lax.div(p, 2) * (1 - 2 * lax.rem(p, 2))


def iota(shape, dim):
    return lax.broadcasted_iota(jnp.int32, shape, dim)


def split3(x):
    hi = x.astype(BF16)
    rest = x - hi.astype(F32)
    mid = rest.astype(BF16)
    low = (rest - mid.astype(F32)).astype(BF16)
    return jnp.concatenate([hi, mid, low], axis=0)


def exact_move(x, pick):
    rows = x.shape[0]
    y = jnp.dot(split3(x), pick, preferred_element_type=F32)
    return y[:rows] + y[rows : 2 * rows] + y[2 * rows :]


def from_west(x):
    axis, n = x.ndim - 1, x.shape[-1]
    even, odd = x[..., : n // 2], x[..., n // 2 :]
    return jnp.concatenate([pltpu.roll(odd, 1, axis), even], axis=axis)


def from_east(x):
    axis, n = x.ndim - 1, x.shape[-1]
    even, odd = x[..., : n // 2], x[..., n // 2 :]
    return jnp.concatenate([odd, pltpu.roll(even, n // 2 - 1, axis)], axis=axis)


def fine_sweep(state, force):
    cur = state
    rows = cur.shape[1]
    fields = cur.shape[0] // 2
    for _ in range(FINE):
        north = pltpu.roll(cur, 1, 1)
        south = pltpu.roll(cur, rows - 1, 1)
        down = (south - north) * 0.5
        vert = south + north - 4.0 * cur
        out = [None] * (2 * fields)
        for b in (0, 1):
            across, lap = [], []
            for f in range(fields):
                ev, od = cur[2 * f], cur[2 * f + 1]
                if b == 0:
                    east, west = od, from_west(od)
                else:
                    east, west = from_east(ev), ev
                across.append((east - west) * 0.5)
                lap.append(vert[2 * f + b] + east + west)
            u, v = cur[b], cur[2 + b]

            def carried(f):
                return u * across[f] + v * down[2 * f + b]

            rates = [
                VISCOSITY * lap[0] - carried(0) - across[2] + force[b],
                VISCOSITY * lap[1] - carried(1) - down[4 + b] + force[2 + b],
                VISCOSITY * lap[2] - (across[0] + down[2 + b]),
                DIFFUSIVITY * lap[3] - carried(3),
            ]
            for f in range(fields):
                out[2 * f + b] = cur[2 * f + b] + TIME_STEP * rates[f]
        cur = jnp.stack(out)
    return cur


def gelu(x):
    half = 0.5 * x
    return half + half * jnp.tanh(x * (0.7978845608028654 + 0.035677408136300125 * (x * x)))


def kernel(tm, spaces, ens, u_hbm, f_hbm, wd_hbm, dk_hbm, wp_hbm, wu_hbm, out_ref, mean_ref,
           u_in, f_in, wd_ref, dk_ref, wp_ref, wu_ref,
           pick, wd4, wu4, wcs, near, snd_w, nrt_w, sth_w, snd, nrt, sth,
           ebuf, got,
           load_sem, near_send, near_recv, far_send, far_recv, send_sem, recv_sem,
           end_send, end_recv, reach):
    loads = []
    for i, (src, dst) in enumerate([(u_hbm, u_in), (f_hbm, f_in), (wd_hbm, wd_ref), (dk_hbm, dk_ref),
                                    (wp_hbm, wp_ref), (wu_hbm, wu_ref)]):
        loads.append(pltpu.make_async_copy(src, dst, load_sem.at[i]))
    for c in loads:
        c.start()
    e = lax.axis_index("ens")
    t = lax.axis_index("tm")
    s = lax.axis_index("space")
    _, fields, half, columns = u_in.shape
    cols = columns // 2
    block = half // tm
    ch = wd_ref.shape[1]
    layers = wp_ref.shape[0]
    groups = 2 * fields
    count = groups + 2 * f_in.shape[0]
    wide = groups * block
    pos = swap_order(t)
    pair, core = lax.div(s, 2), lax.rem(s, 2)
    pairs, ring = spaces // 2, 2 * tm
    own = 2 * pos + core

    def at_block(g):
        g = lax.rem(g, pairs * ring)
        q, b = lax.div(g, ring), lax.rem(g, ring)
        return {"tm": swap_order(lax.div(b, 2)), "space": 2 * q + lax.rem(b, 2)}

    to_north = at_block(pair * ring + own + pairs * ring - 1)
    to_south = at_block(pair * ring + own + 1)

    barrier = pltpu.get_barrier_semaphore()
    plane = [at_block(pair * ring + lax.rem(own + i, ring)) for i in range(1, ring)]
    peers = plane + [{"ens": lax.rem(e + i, ens)} for i in range(1, ens)]
    beside = []
    for turn in ((pairs - 1, 1) if pairs > 1 else ()):
        for c in (0, 1):
            beside.append({"space": 2 * lax.rem(pair + turn, pairs) + c})
    expected = len(peers) + len(beside)
    for peer in peers + beside:
        pl.semaphore_signal(barrier, inc=1, device_id=peer, device_id_type=MESH)
    if pairs > 1:
        for edge, across in ((0, to_north), (ring - 1, to_south)):
            @pl.when(own == edge)
            def _():
                pl.semaphore_signal(barrier, inc=1, device_id=across, device_id_type=MESH)
        expected = expected + jnp.where((own == 0) | (own == ring - 1), 1, 0)

    quarter = columns // 4
    lane = iota((1, columns), 1)
    column = 4 * lax.rem(lane, quarter) + 2 * lax.rem(lax.div(lane, quarter), 2) + lax.div(lane, 2 * quarter)
    pick[...] = jnp.where(iota((columns, columns), 0) == column, 1.0, 0.0).astype(BF16)
    loads[0].wait()
    loads[1].wait()
    both = jnp.concatenate([u_in[0].reshape(fields * half, columns), f_in[...].reshape(-1, columns)], axis=0)
    moved = exact_move(both, pick[...]).reshape(count // 2, half, columns)
    for k in range(tm):
        rows = moved[:, k * block : (k + 1) * block]
        two = jnp.stack([rows[..., :cols], rows[..., cols:]], axis=1)
        near[core * tm + k] = two.reshape(count * block, cols)

    pl.semaphore_wait(barrier, expected)
    mine = near.at[pl.ds(core * tm, tm)]
    swap = pltpu.make_async_remote_copy(mine, mine, near_send, near_recv,
                                        device_id={"space": 2 * pair + 1 - core}, device_id_type=MESH)
    swap.start()
    if pairs > 1:
        edge = near.at[pl.ds(core * (ring - 2), 2)]
        there = 2 * lax.rem(pair + pairs - 1 + 2 * core, pairs)
        far = [pltpu.make_async_remote_copy(edge, near.at[pl.ds(ring + 2 * core, 2)], far_send.at[c], far_recv.at[core],
                                            device_id={"space": there + c}, device_id_type=MESH) for c in (0, 1)]
        for c in far:
            c.start()
    for peer in plane:
        pl.semaphore_signal(reach, inc=1, device_id=peer, device_id_type=MESH)

    for c in loads[2:]:
        c.wait()
    for h in range(block // 2):
        q, k = iota((wide, 2 * groups), 1), iota((wide, 2 * groups), 0)
        fq, aq, bq = q // 4, (q // 2) % 2, q % 2
        gk, rk = k // block, k % block
        sel = jnp.where((gk == 2 * fq + bq) & (rk == 2 * h + aq), 1.0, 0.0).astype(BF16)
        wu4[:, h * ch : (h + 1) * ch] = jnp.dot(sel, wu_ref[...], preferred_element_type=F32).astype(BF16)
        wd4[h * ch : (h + 1) * ch] = jnp.dot(sel, wd_ref[...], preferred_element_type=F32).T.astype(BF16)
    for l in range(layers):
        w = wp_ref[l].astype(F32)
        for a in range(3):
            for b in range(3):
                tap = dk_ref[3 * a + b, l : l + 1, :]
                wcs[l, b * ch : (b + 1) * ch, a * ch : (a + 1) * ch] = (w * tap).astype(BF16)

    def coarse(tasks):
        n_in = len(tasks[0])
        rows = []
        for k in range(n_in):
            x = jnp.concatenate([task[k].astype(BF16) for task in tasks], axis=1)
            rows.append(jnp.dot(wd4[...], x, preferred_element_type=F32).astype(BF16))
        hidden = jnp.concatenate(rows, axis=0)
        width = hidden.shape[1]
        for l in range(layers):
            n_out = hidden.shape[0] // ch - 2
            new = []
            for r in range(n_out):
                y = jnp.dot(wcs[l], hidden[r * ch : (r + 3) * ch], preferred_element_type=F32)
                lifted = []
                for c in range(0, width, cols):
                    lifted.append(y[ch : 2 * ch, c : c + cols] + from_west(y[:ch, c : c + cols])
                                  + from_east(y[2 * ch :, c : c + cols]))
                lifted = jnp.concatenate(lifted, axis=1)
                old = hidden[(r + 1) * ch : (r + 2) * ch].astype(F32)
                new.append((old + gelu(lifted)).astype(BF16))
            hidden = jnp.concatenate(new, axis=0)
        deltas = []
        for k in range(n_in - 2):
            deltas.append(jnp.dot(wu4[...], hidden[2 * k * ch : 2 * (k + 1) * ch], preferred_element_type=F32))
        return [[d[:, i * cols : (i + 1) * cols] for d in deltas] for i in range(len(tasks))]

    def in_rows(pieces):
        pieces = [p.astype(F32).reshape(-1, block, cols) for p in pieces]
        if len(pieces) * block % 8:
            pieces.append(jnp.zeros_like(pieces[0]))
        return jnp.concatenate(pieces, axis=1)

    def fine(pieces, force):
        done = fine_sweep(in_rows(pieces), force)
        return [done[:, (k + 1) * block : (k + 2) * block].reshape(wide, cols) for k in range(len(pieces) - 2)]

    def exchange(i, src, from_north, from_south):
        copies = [
            pltpu.make_async_remote_copy(src, from_south, send_sem.at[i, 0], recv_sem.at[i, 0],
                                         device_id=to_north, device_id_type=MESH),
            pltpu.make_async_remote_copy(src, from_north, send_sem.at[i, 1], recv_sem.at[i, 1],
                                         device_id=to_south, device_id_type=MESH),
        ]
        for c in copies:
            c.start()
        return copies

    row_place = lax.rem(own, tm)
    keeper = 2 * pair + lax.div(own, tm)

    def finish(n, end):
        x = end.astype(BF16).astype(F32).reshape(fields, 2, block, cols)
        flat = jnp.concatenate([x[:, 0].reshape(-1, cols), x[:, 1].reshape(-1, cols)], axis=1).astype(BF16)
        line = lax.dot_general(flat, pick[...], (((1,), (1,)), ((), ())), preferred_element_type=F32).astype(BF16)
        ebuf[n] = line
        for d in range(1, ens):
            end_copy(n, d).start()
        here = (t == n) & (s == keeper)

        @pl.when(here)
        def _():
            pltpu.make_async_copy(ebuf.at[n], got.at[e, row_place], end_recv).start()

        @pl.when(jnp.logical_not(here))
        def _():
            end_copy(n, 0).start()

    def end_copy(n, d):
        return pltpu.make_async_remote_copy(
            ebuf.at[n], got.at[e, row_place], end_send.at[n, d], end_recv,
            device_id={"tm": n, "space": keeper, "ens": lax.rem(e + d, ens)}, device_id_type=MESH)

    def sent(n):
        for d in range(1, ens):
            end_copy(n, d).wait_send()

        @pl.when((t != n) | (s != keeper))
        def _():
            end_copy(n, 0).wait_send()

    def collect():
        for n in range(tm):
            sent(n)
        pltpu.make_async_copy(got, got, end_recv).wait()
        for p in range(tm):
            total = got[0, p].astype(F32)
            for d in range(1, ens):
                total = total + got[d, p].astype(F32)
            out_ref[:, p * block : (p + 1) * block] = got[e, p].astype(F32).reshape(fields, block, columns)
            mean_ref[:, p * block : (p + 1) * block] = (total * (1.0 / ens)).reshape(fields, block, columns)

    swap.wait()
    if pairs > 1:
        for c in (0, 1):
            far[c].wait_send()
            pltpu.make_async_copy(near.at[pl.ds(0, 2)], near.at[pl.ds(ring + 2 * c, 2)], far_recv.at[c]).wait()
    depth = near.shape[0]
    everything = [near[lax.rem(own + depth - 2 + k, depth)] for k in range(5)]
    start = [x[:wide] for x in everything]
    force = in_rows([x[wide:] for x in everything])
    force_near = in_rows([x[wide:] for x in everything[1:4]])

    v1 = fine(start, force)
    u1 = [x + d for x, d in zip(start[1:4], coarse([start])[0])]

    w2 = fine(v1, force_near)[0]
    snd_w[...] = w2.astype(BF16)
    moving_w = exchange(0, snd_w, nrt_w, sth_w)
    fu1 = fine(u1, force_near)[0]
    du1, dv1 = coarse([u1, v1])
    u2 = u1[1] + du1[0]
    v2 = v1[1] + dv1[0] + (fu1 - u2)
    snd[0, 0] = u2.astype(BF16)
    snd[0, 1] = v2.astype(BF16)
    moving = exchange(1, snd.at[0], nrt.at[0], sth.at[0])
    pl.semaphore_wait(reach, len(plane))
    finish(0, v1[1])
    finish(1, w2)
    for c in moving_w + moving:
        c.wait()
    u2p = [nrt[0, 0], u2, sth[0, 0]]
    v2p = [nrt[0, 1], v2, sth[0, 1]]
    w2p = [nrt_w[...], w2, sth_w[...]]

    fu2 = fine(u2p, force_near)[0]
    fv2 = fine(v2p, force_near)[0]
    du2, dv2, dw2 = coarse([u2p, v2p, w2p])
    gv2 = v2 + dv2[0]
    v3 = gv2 + (fu2 - (u2 + du2[0]))
    w3 = w2 + dw2[0] + (fv2 - gv2)
    snd[1, 0] = v3.astype(BF16)
    snd[1, 1] = w3.astype(BF16)
    moving = exchange(2, snd.at[1], nrt.at[1], sth.at[1])
    finish(2, w3)
    for c in moving:
        c.wait()
    v3p = [nrt[1, 0], v3, sth[1, 0]]
    w3p = [nrt[1, 1], w3, sth[1, 1]]

    fv3 = fine(v3p, force_near)[0]
    dv3, dw3 = coarse([v3p, w3p])
    finish(3, w3 + dw3[0] + (fv3 - (v3 + dv3[0])))
    collect()


def local(initial_state, forcing, w_down, depth_kernel, w_point, w_up):
    tm, spaces, ens = lax.axis_size("tm"), lax.axis_size("space"), lax.axis_size("ens")
    _, fields, half, columns = initial_state.shape
    block = half // tm
    cols, groups = columns // 2, 2 * fields
    layers, ch, _ = depth_kernel.shape
    assert block == FINE == 2 * layers and tm == 4
    assert spaces % 2 == 0 and columns % 512 == 0
    count = groups + 2 * forcing.shape[0]
    near = 2 * tm + (4 if spaces > 2 else 0)
    vmem = pl.BlockSpec(memory_space=pltpu.VMEM)
    hbm = pl.BlockSpec(memory_space=pltpu.HBM)
    args = (initial_state, forcing, w_down.T, depth_kernel.transpose(2, 0, 1), w_point, w_up)
    args = tuple(pltpu.with_memory_space_constraint(a, pltpu.HBM) for a in args)
    ending, mean = pl.pallas_call(
        lambda *refs: kernel(tm, spaces, ens, *refs),
        name="parareal",
        out_shape=[pltpu.VMEM((fields, half, columns), F32)] * 2,
        in_specs=[hbm] * 6,
        out_specs=[vmem] * 2,
        scratch_shapes=[pltpu.VMEM(a.shape, a.dtype) for a in args] + [
            pltpu.VMEM((columns, columns), BF16),
            pltpu.VMEM((2 * ch, groups * block), BF16),
            pltpu.VMEM((groups * block, 2 * ch), BF16),
            pltpu.VMEM((layers, 3 * ch, 3 * ch), BF16),
            pltpu.VMEM((near, count * block, cols), F32),
            pltpu.VMEM((groups * block, cols), BF16),
            pltpu.VMEM((groups * block, cols), BF16),
            pltpu.VMEM((groups * block, cols), BF16),
            pltpu.VMEM((2, 2, groups * block, cols), BF16),
            pltpu.VMEM((2, 2, groups * block, cols), BF16),
            pltpu.VMEM((2, 2, groups * block, cols), BF16),
            pltpu.VMEM((tm, fields * block, columns), BF16),
            pltpu.VMEM((ens, tm, fields * block, columns), BF16),
            pltpu.SemaphoreType.DMA((6,)),
            pltpu.SemaphoreType.DMA,
            pltpu.SemaphoreType.DMA,
            pltpu.SemaphoreType.DMA((2,)),
            pltpu.SemaphoreType.DMA((2,)),
            pltpu.SemaphoreType.DMA((3, 2)),
            pltpu.SemaphoreType.DMA((3, 2)),
            pltpu.SemaphoreType.DMA((tm, ens)),
            pltpu.SemaphoreType.DMA,
            pltpu.SemaphoreType.REGULAR,
        ],
        compiler_params=pltpu.CompilerParams(has_side_effects=True, collective_id=0, vmem_limit_bytes=40 << 20),
    )(*args)
    return ending[None, None], mean[None]


def solution(mesh):
    in_specs = (P("ens", None, "space", None), P(None, "space", None), P(), P(), P(), P())
    out_specs = (P("ens", "tm", None, "space", None), P("tm", None, "space", None))
    return jax.shard_map(local, mesh=mesh, in_specs=in_specs, out_specs=out_specs, check_vma=False)
```

```python
import jax
import jax.numpy as jnp
from jax import lax
from jax.experimental import pallas as pl
from jax.experimental.pallas import tpu as pltpu
from jax.sharding import PartitionSpec as P

TIME_STEP = 0.05
VISCOSITY = 0.5
DIFFUSIVITY = 0.3
FINE = 4
MESH = pl.DeviceIdType.MESH
F32 = jnp.float32
BF16 = jnp.bfloat16


def swap_order(p):
    return p + lax.div(p, 2) * (1 - 2 * lax.rem(p, 2))


def iota(shape, dim):
    return lax.broadcasted_iota(jnp.int32, shape, dim)


def split3(x):
    hi = x.astype(BF16)
    rest = x - hi.astype(F32)
    mid = rest.astype(BF16)
    low = (rest - mid.astype(F32)).astype(BF16)
    return jnp.concatenate([hi, mid, low], axis=0)


def exact_move(x, pick):
    rows = x.shape[0]
    y = jnp.dot(split3(x), pick, preferred_element_type=F32)
    return y[:rows] + y[rows : 2 * rows] + y[2 * rows :]


def from_west(x):
    axis, n = x.ndim - 1, x.shape[-1]
    even, odd = x[..., : n // 2], x[..., n // 2 :]
    return jnp.concatenate([pltpu.roll(odd, 1, axis), even], axis=axis)


def from_east(x):
    axis, n = x.ndim - 1, x.shape[-1]
    even, odd = x[..., : n // 2], x[..., n // 2 :]
    return jnp.concatenate([odd, pltpu.roll(even, n // 2 - 1, axis)], axis=axis)


def fine_sweep(state, force):
    cur = state
    rows = cur.shape[1]
    fields = cur.shape[0] // 2
    for _ in range(FINE):
        north = pltpu.roll(cur, 1, 1)
        south = pltpu.roll(cur, rows - 1, 1)
        down = (south - north) * 0.5
        vert = south + north - 4.0 * cur
        out = [None] * (2 * fields)
        for b in (0, 1):
            across, lap = [], []
            for f in range(fields):
                ev, od = cur[2 * f], cur[2 * f + 1]
                if b == 0:
                    east, west = od, from_west(od)
                else:
                    east, west = from_east(ev), ev
                across.append((east - west) * 0.5)
                lap.append(vert[2 * f + b] + east + west)
            u, v = cur[b], cur[2 + b]

            def carried(f):
                return u * across[f] + v * down[2 * f + b]

            rates = [
                VISCOSITY * lap[0] - carried(0) - across[2] + force[b],
                VISCOSITY * lap[1] - carried(1) - down[4 + b] + force[2 + b],
                VISCOSITY * lap[2] - (across[0] + down[2 + b]),
                DIFFUSIVITY * lap[3] - carried(3),
            ]
            for f in range(fields):
                out[2 * f + b] = cur[2 * f + b] + TIME_STEP * rates[f]
        cur = jnp.stack(out)
    return cur


def gelu(x):
    half = 0.5 * x
    return half + half * jnp.tanh(x * (0.7978845608028654 + 0.035677408136300125 * (x * x)))


def kernel(tm, spaces, ens, u_hbm, f_hbm, wd_hbm, dk_hbm, wp_hbm, wu_hbm, both_ref,
           u_in, f_in, wd_ref, dk_ref, wp_ref, wu_ref,
           pick, wd4, wu4, wcs, near, snd_w, nrt_w, sth_w, snd, nrt, sth,
           ebuf, got,
           load_sem, near_send, near_recv, far_send, far_recv, send_sem, recv_sem,
           end_send, end_recv, reach):
    loads = []
    for i, (src, dst) in enumerate([(u_hbm, u_in), (f_hbm, f_in), (wd_hbm, wd_ref), (dk_hbm, dk_ref),
                                    (wp_hbm, wp_ref), (wu_hbm, wu_ref)]):
        loads.append(pltpu.make_async_copy(src, dst, load_sem.at[i]))
    for c in loads:
        c.start()
    e = lax.axis_index("ens")
    t = lax.axis_index("tm")
    s = lax.axis_index("space")
    _, fields, half, columns = u_in.shape
    cols = columns // 2
    block = half // tm
    ch = wd_ref.shape[1]
    layers = wp_ref.shape[0]
    groups = 2 * fields
    count = groups + 2 * f_in.shape[0]
    wide = groups * block
    pos = swap_order(t)
    pair, core = lax.div(s, 2), lax.rem(s, 2)
    pairs, ring = spaces // 2, 2 * tm
    own = 2 * pos + core

    def at_block(g):
        g = lax.rem(g, pairs * ring)
        q, b = lax.div(g, ring), lax.rem(g, ring)
        return {"tm": swap_order(lax.div(b, 2)), "space": 2 * q + lax.rem(b, 2)}

    to_north = at_block(pair * ring + own + pairs * ring - 1)
    to_south = at_block(pair * ring + own + 1)

    def around(step):
        return at_block(pair * ring + lax.rem(own + ring + step, ring))

    def greet(sem, step):
        for sign in (-1, 1):
            pl.semaphore_signal(sem, inc=1, device_id=around(sign * step), device_id_type=MESH)
            other = e + sign * step

            @pl.when((core == 1) & (other >= 0) & (other < ens))
            def _():
                pl.semaphore_signal(sem, inc=1, device_id={"ens": other}, device_id_type=MESH)

    def greetings(step):
        line = jnp.where(e >= step, 1, 0) + jnp.where(e + step < ens, 1, 0)
        return 2 + core * line

    barrier = pltpu.get_barrier_semaphore()
    plane = [around(i) for i in range(1, ring)]
    beside = []
    for turn in ((pairs - 1, 1) if pairs > 1 else ()):
        for c in (0, 1):
            beside.append({"space": 2 * lax.rem(pair + turn, pairs) + c})
    greet(barrier, 1)
    expected = greetings(1) + len(beside)
    for peer in beside:
        pl.semaphore_signal(barrier, inc=1, device_id=peer, device_id_type=MESH)
    if pairs > 1:
        for edge, across in ((0, to_north), (ring - 1, to_south)):
            @pl.when(own == edge)
            def _():
                pl.semaphore_signal(barrier, inc=1, device_id=across, device_id_type=MESH)
        expected = expected + jnp.where((own == 0) | (own == ring - 1), 1, 0)

    quarter = columns // 4
    lane = iota((1, columns), 1)
    column = 4 * lax.rem(lane, quarter) + 2 * lax.rem(lax.div(lane, quarter), 2) + lax.div(lane, 2 * quarter)
    pick[...] = jnp.where(iota((columns, columns), 0) == column, 1.0, 0.0).astype(BF16)
    loads[0].wait()
    loads[1].wait()
    both = jnp.concatenate([u_in[0].reshape(fields * half, columns), f_in[...].reshape(-1, columns)], axis=0)
    moved = exact_move(both, pick[...]).reshape(count // 2, half, columns)
    for k in range(tm):
        rows = moved[:, k * block : (k + 1) * block]
        two = jnp.stack([rows[..., :cols], rows[..., cols:]], axis=1)
        near[core * tm + k] = two.reshape(count * block, cols)

    pl.semaphore_wait(barrier, expected)
    mine = near.at[pl.ds(core * tm, tm)]
    swap = pltpu.make_async_remote_copy(mine, mine, near_send, near_recv,
                                        device_id={"space": 2 * pair + 1 - core}, device_id_type=MESH)
    swap.start()
    if pairs > 1:
        edge = near.at[pl.ds(core * (ring - 2), 2)]
        there = 2 * lax.rem(pair + pairs - 1 + 2 * core, pairs)
        far = [pltpu.make_async_remote_copy(edge, near.at[pl.ds(ring + 2 * core, 2)], far_send.at[c], far_recv.at[core],
                                            device_id={"space": there + c}, device_id_type=MESH) for c in (0, 1)]
        for c in far:
            c.start()
    greet(reach.at[0], 1)

    for c in loads[2:]:
        c.wait()
    for h in range(block // 2):
        q, k = iota((wide, 2 * groups), 1), iota((wide, 2 * groups), 0)
        fq, aq, bq = q // 4, (q // 2) % 2, q % 2
        gk, rk = k // block, k % block
        sel = jnp.where((gk == 2 * fq + bq) & (rk == 2 * h + aq), 1.0, 0.0).astype(BF16)
        wu4[:, h * ch : (h + 1) * ch] = jnp.dot(sel, wu_ref[...], preferred_element_type=F32).astype(BF16)
        wd4[h * ch : (h + 1) * ch] = jnp.dot(sel, wd_ref[...], preferred_element_type=F32).T.astype(BF16)
    for l in range(layers):
        w = wp_ref[l].astype(F32)
        for a in range(3):
            for b in range(3):
                tap = dk_ref[3 * a + b, l : l + 1, :]
                wcs[l, b * ch : (b + 1) * ch, a * ch : (a + 1) * ch] = (w * tap).astype(BF16)

    def down(pieces):
        x = jnp.concatenate([p.astype(BF16) for p in pieces], axis=1)
        return jnp.dot(wd4[...], x, preferred_element_type=F32).astype(BF16)

    def conv(l, a, x):
        y = jnp.dot(wcs[l, :, a * ch : a * ch + x.shape[0]], x, preferred_element_type=F32)
        lifted = []
        for c in range(0, x.shape[1], cols):
            lifted.append(y[ch : 2 * ch, c : c + cols] + from_west(y[:ch, c : c + cols])
                          + from_east(y[2 * ch :, c : c + cols]))
        return jnp.concatenate(lifted, axis=1)

    def mixed(old, lifted):
        return (old.astype(F32) + gelu(lifted)).astype(BF16)

    def blocks(hidden, first):
        for l in range(first, layers):
            new = []
            for r in range(hidden.shape[0] // ch - 2):
                new.append(mixed(hidden[(r + 1) * ch : (r + 2) * ch], conv(l, 0, hidden[r * ch : (r + 3) * ch])))
            hidden = jnp.concatenate(new, axis=0)
        deltas = []
        for r in range(0, hidden.shape[0], 2 * ch):
            deltas.append(jnp.dot(wu4[...], hidden[r : r + 2 * ch], preferred_element_type=F32))
        return [[d[:, c : c + cols] for d in deltas] for c in range(0, hidden.shape[1], cols)]

    def coarse(tasks):
        return blocks(jnp.concatenate([down(pieces) for pieces in zip(*tasks)], axis=0), 0)

    def coarse_own(own_pieces):
        h = down(own_pieces)
        return h, [conv(0, 2, h[:ch]), conv(0, 1, h), conv(0, 0, h), conv(0, 0, h[ch:])]

    def coarse_rest(begun, norths, souths):
        h, part = begun
        hn, hs = down(norths), down(souths)
        new = [
            mixed(hn[ch:], part[0] + conv(0, 0, hn)),
            mixed(h[:ch], part[1] + conv(0, 0, hn[ch:])),
            mixed(h[ch:], part[2] + conv(0, 2, hs[:ch])),
            mixed(hs[:ch], part[3] + conv(0, 1, hs)),
        ]
        return [d[0] for d in blocks(jnp.concatenate(new, axis=0), 1)]

    def in_rows(pieces):
        pieces = [p.astype(F32).reshape(-1, block, cols) for p in pieces]
        if len(pieces) * block % 8:
            pieces.append(jnp.zeros_like(pieces[0]))
        return jnp.concatenate(pieces, axis=1)

    def fine(pieces, force):
        done = fine_sweep(in_rows(pieces), force)
        return [done[:, (k + 1) * block : (k + 2) * block].reshape(wide, cols) for k in range(len(pieces) - 2)]

    def exchange(i, src, from_north, from_south):
        copies = [
            pltpu.make_async_remote_copy(src, from_south, send_sem.at[i, 0], recv_sem.at[i, 0],
                                         device_id=to_north, device_id_type=MESH),
            pltpu.make_async_remote_copy(src, from_north, send_sem.at[i, 1], recv_sem.at[i, 1],
                                         device_id=to_south, device_id_type=MESH),
        ]
        for c in copies:
            c.start()
        return copies

    row_place = lax.rem(own, tm)
    keeper = 2 * pair + lax.div(own, tm)

    def finish(n, end):
        x = end.astype(BF16).astype(F32).reshape(fields, 2, block, cols)
        flat = jnp.concatenate([x[:, 0].reshape(-1, cols), x[:, 1].reshape(-1, cols)], axis=1).astype(BF16)
        line = lax.dot_general(flat, pick[...], (((1,), (1,)), ((), ())), preferred_element_type=F32).astype(BF16)
        ebuf[n] = line
        for d in range(1, ens):
            end_copy(n, d).start()
        here = (t == n) & (s == keeper)

        @pl.when(here)
        def _():
            pltpu.make_async_copy(ebuf.at[n], got.at[e, row_place], end_recv).start()

        @pl.when(jnp.logical_not(here))
        def _():
            end_copy(n, 0).start()

    def end_copy(n, d):
        return pltpu.make_async_remote_copy(
            ebuf.at[n], got.at[e, row_place], end_send.at[n, d], end_recv,
            device_id={"tm": n, "space": keeper, "ens": lax.rem(e + d, ens)}, device_id_type=MESH)

    def sent(n):
        for d in range(1, ens):
            end_copy(n, d).wait_send()

        @pl.when((t != n) | (s != keeper))
        def _():
            end_copy(n, 0).wait_send()

    def collect():
        for n in range(tm):
            sent(n)
        pltpu.make_async_copy(got, got, end_recv).wait()
        for p in range(tm):
            total = got[0, p].astype(F32)
            for d in range(1, ens):
                total = total + got[d, p].astype(F32)
            both_ref[0, :, p * block : (p + 1) * block] = got[e, p].astype(F32).reshape(fields, block, columns)
            both_ref[1, :, p * block : (p + 1) * block] = (total * (1.0 / ens)).reshape(fields, block, columns)

    swap.wait()
    if pairs > 1:
        for c in (0, 1):
            far[c].wait_send()
            pltpu.make_async_copy(near.at[pl.ds(0, 2)], near.at[pl.ds(ring + 2 * c, 2)], far_recv.at[c]).wait()
    depth = near.shape[0]
    everything = [near[lax.rem(own + depth - 2 + k, depth)] for k in range(5)]
    start = [x[:wide] for x in everything]
    force = in_rows([x[wide:] for x in everything])
    force_near = in_rows([x[wide:] for x in everything[1:4]])

    v1 = fine(start, force)
    w2 = fine(v1, force_near)[0]
    u1 = [x + d for x, d in zip(start[1:4], coarse([start])[0])]
    snd_w[...] = w2.astype(BF16)
    moving_w = exchange(0, snd_w, nrt_w, sth_w)
    pl.semaphore_wait(reach.at[0], greetings(1))
    greet(reach.at[1], 2)

    fu1 = fine(u1, force_near)[0]
    du1, dv1 = coarse([u1, v1])
    u2 = u1[1] + du1[0]
    v2 = v1[1] + dv1[0] + (fu1 - u2)
    snd[0, 0] = u2.astype(BF16)
    snd[0, 1] = v2.astype(BF16)
    moving = exchange(1, snd.at[0], nrt.at[0], sth.at[0])
    pl.semaphore_wait(reach.at[1], greetings(2))
    for peer in plane:
        pl.semaphore_signal(reach.at[2], inc=1, device_id=peer, device_id_type=MESH)
    begun = coarse_own([u2, v2])
    for c in moving_w:
        c.wait()
    gw2 = w2 + coarse([[nrt_w[...], w2, sth_w[...]]])[0][0]
    pl.semaphore_wait(reach.at[2], len(plane))
    finish(0, v1[1])
    finish(1, w2)
    for c in moving:
        c.wait()
    fu2 = fine([nrt[0, 0], u2, sth[0, 0]], force_near)[0]
    fv2 = fine([nrt[0, 1], v2, sth[0, 1]], force_near)[0]
    du2, dv2 = coarse_rest(begun, [nrt[0, 0], nrt[0, 1]], [sth[0, 0], sth[0, 1]])
    gv2 = v2 + dv2
    v3 = gv2 + (fu2 - (u2 + du2))
    w3 = gw2 + (fv2 - gv2)
    snd[1, 0] = v3.astype(BF16)
    snd[1, 1] = w3.astype(BF16)
    moving = exchange(2, snd.at[1], nrt.at[1], sth.at[1])
    begun = coarse_own([v3, w3])
    for c in moving:
        c.wait()
    finish(2, w3)
    fv3 = fine([nrt[1, 0], v3, sth[1, 0]], force_near)[0]
    dv3, dw3 = coarse_rest(begun, [nrt[1, 0], nrt[1, 1]], [sth[1, 0], sth[1, 1]])
    finish(3, w3 + dw3 + (fv3 - (v3 + dv3)))
    collect()


def local(initial_state, forcing, w_down, depth_kernel, w_point, w_up):
    tm, spaces, ens = lax.axis_size("tm"), lax.axis_size("space"), lax.axis_size("ens")
    _, fields, half, columns = initial_state.shape
    block = half // tm
    cols, groups = columns // 2, 2 * fields
    layers, ch, _ = depth_kernel.shape
    assert block == FINE == 2 * layers == 4 and tm == 4
    assert spaces % 2 == 0 and ens <= 4 and columns % 512 == 0
    count = groups + 2 * forcing.shape[0]
    near = 2 * tm + (4 if spaces > 2 else 0)
    vmem = pl.BlockSpec(memory_space=pltpu.VMEM)
    hbm = pl.BlockSpec(memory_space=pltpu.HBM)
    args = (initial_state, forcing, w_down.T, depth_kernel.transpose(2, 0, 1), w_point, w_up)
    args = tuple(pltpu.with_memory_space_constraint(a, pltpu.HBM) for a in args)
    both = pl.pallas_call(
        lambda *refs: kernel(tm, spaces, ens, *refs),
        name="parareal",
        out_shape=pltpu.VMEM((2, fields, half, columns), F32),
        in_specs=[hbm] * 6,
        out_specs=vmem,
        scratch_shapes=[pltpu.VMEM(a.shape, a.dtype) for a in args] + [
            pltpu.VMEM((columns, columns), BF16),
            pltpu.VMEM((2 * ch, groups * block), BF16),
            pltpu.VMEM((groups * block, 2 * ch), BF16),
            pltpu.VMEM((layers, 3 * ch, 3 * ch), BF16),
            pltpu.VMEM((near, count * block, cols), F32),
            pltpu.VMEM((groups * block, cols), BF16),
            pltpu.VMEM((groups * block, cols), BF16),
            pltpu.VMEM((groups * block, cols), BF16),
            pltpu.VMEM((2, 2, groups * block, cols), BF16),
            pltpu.VMEM((2, 2, groups * block, cols), BF16),
            pltpu.VMEM((2, 2, groups * block, cols), BF16),
            pltpu.VMEM((tm, fields * block, columns), BF16),
            pltpu.VMEM((ens, tm, fields * block, columns), BF16),
            pltpu.SemaphoreType.DMA((6,)),
            pltpu.SemaphoreType.DMA,
            pltpu.SemaphoreType.DMA,
            pltpu.SemaphoreType.DMA((2,)),
            pltpu.SemaphoreType.DMA((2,)),
            pltpu.SemaphoreType.DMA((3, 2)),
            pltpu.SemaphoreType.DMA((3, 2)),
            pltpu.SemaphoreType.DMA((tm, ens)),
            pltpu.SemaphoreType.DMA,
            pltpu.SemaphoreType.REGULAR((3,)),
        ],
        compiler_params=pltpu.CompilerParams(has_side_effects=True, collective_id=0, vmem_limit_bytes=40 << 20),
    )(*args)
    return both[0][None, None], both[1][None]


def solution(mesh):
    in_specs = (P("ens", None, "space", None), P(None, "space", None), P(), P(), P(), P())
    out_specs = (P("ens", "tm", None, "space", None), P("tm", None, "space", None))
    return jax.shard_map(local, mesh=mesh, in_specs=in_specs, out_specs=out_specs, check_vma=False)
```

```python
import jax
import jax.numpy as jnp
from jax import lax
from jax.experimental import pallas as pl
from jax.experimental.pallas import tpu as pltpu
from jax.sharding import PartitionSpec as P

TIME_STEP = 0.05
VISCOSITY = 0.5
DIFFUSIVITY = 0.3
FINE = 4
MESH = pl.DeviceIdType.MESH
F32 = jnp.float32
BF16 = jnp.bfloat16


def swap_order(p):
    return p + lax.div(p, 2) * (1 - 2 * lax.rem(p, 2))


def iota(shape, dim):
    return lax.broadcasted_iota(jnp.int32, shape, dim)


def split3(x):
    hi = x.astype(BF16)
    rest = x - hi.astype(F32)
    mid = rest.astype(BF16)
    low = (rest - mid.astype(F32)).astype(BF16)
    return jnp.concatenate([hi, mid, low], axis=0)


def exact_move(x, pick):
    rows = x.shape[0]
    y = jnp.dot(split3(x), pick, preferred_element_type=F32)
    return y[:rows] + y[rows : 2 * rows] + y[2 * rows :]


def from_west(x):
    axis, n = x.ndim - 1, x.shape[-1]
    even, odd = x[..., : n // 2], x[..., n // 2 :]
    return jnp.concatenate([pltpu.roll(odd, 1, axis), even], axis=axis)


def from_east(x):
    axis, n = x.ndim - 1, x.shape[-1]
    even, odd = x[..., : n // 2], x[..., n // 2 :]
    return jnp.concatenate([odd, pltpu.roll(even, n // 2 - 1, axis)], axis=axis)


def fine_sweep(state, force):
    cur = state
    rows = cur.shape[1]
    fields = cur.shape[0] // 2
    for _ in range(FINE):
        north = pltpu.roll(cur, 1, 1)
        south = pltpu.roll(cur, rows - 1, 1)
        down = (south - north) * 0.5
        vert = south + north - 4.0 * cur
        out = [None] * (2 * fields)
        for b in (0, 1):
            across, lap = [], []
            for f in range(fields):
                ev, od = cur[2 * f], cur[2 * f + 1]
                if b == 0:
                    east, west = od, from_west(od)
                else:
                    east, west = from_east(ev), ev
                across.append((east - west) * 0.5)
                lap.append(vert[2 * f + b] + east + west)
            u, v = cur[b], cur[2 + b]

            def carried(f):
                return u * across[f] + v * down[2 * f + b]

            rates = [
                VISCOSITY * lap[0] - carried(0) - across[2] + force[b],
                VISCOSITY * lap[1] - carried(1) - down[4 + b] + force[2 + b],
                VISCOSITY * lap[2] - (across[0] + down[2 + b]),
                DIFFUSIVITY * lap[3] - carried(3),
            ]
            for f in range(fields):
                out[2 * f + b] = cur[2 * f + b] + TIME_STEP * rates[f]
        cur = jnp.stack(out)
    return cur


def gelu(x):
    half = 0.5 * x
    return half + half * jnp.tanh(x * (0.7978845608028654 + 0.035677408136300125 * (x * x)))


def kernel(tm, spaces, ens, u_hbm, f_hbm, wd_hbm, dk_hbm, wp_hbm, wu_hbm, both_ref,
           u_in, f_in, wd_ref, dk_ref, wp_ref, wu_ref,
           pick, place, wd4, wu4, wcs, near, snd_w, nrt_w, sth_w, snd, nrt, sth,
           ebuf, got,
           load_sem, near_send, near_recv, far_send, far_recv, send_sem, recv_sem,
           end_send, end_recv, reach):
    loads = []
    for i, (src, dst) in enumerate([(u_hbm, u_in), (f_hbm, f_in), (wd_hbm, wd_ref), (dk_hbm, dk_ref),
                                    (wp_hbm, wp_ref), (wu_hbm, wu_ref)]):
        loads.append(pltpu.make_async_copy(src, dst, load_sem.at[i]))
    for c in loads:
        c.start()
    e = lax.axis_index("ens")
    t = lax.axis_index("tm")
    s = lax.axis_index("space")
    _, fields, half, columns = u_in.shape
    cols = columns // 2
    block = half // tm
    ch = wd_ref.shape[1]
    layers = wp_ref.shape[0]
    groups = 2 * fields
    count = groups + 2 * f_in.shape[0]
    wide = groups * block
    pos = swap_order(t)
    pair, core = lax.div(s, 2), lax.rem(s, 2)
    pairs, ring = spaces // 2, 2 * tm
    own = 2 * pos + core

    def at_block(g):
        g = lax.rem(g, pairs * ring)
        q, b = lax.div(g, ring), lax.rem(g, ring)
        return {"tm": swap_order(lax.div(b, 2)), "space": 2 * q + lax.rem(b, 2)}

    to_north = at_block(pair * ring + own + pairs * ring - 1)
    to_south = at_block(pair * ring + own + 1)

    def around(step):
        return at_block(pair * ring + lax.rem(own + ring + step, ring))

    def greet(sem, step):
        for sign in (-1, 1):
            pl.semaphore_signal(sem, inc=1, device_id=around(sign * step), device_id_type=MESH)
            other = e + sign * step

            @pl.when((core == 1) & (other >= 0) & (other < ens))
            def _():
                pl.semaphore_signal(sem, inc=1, device_id={"ens": other}, device_id_type=MESH)

    def greetings(step):
        line = jnp.where(e >= step, 1, 0) + jnp.where(e + step < ens, 1, 0)
        return 2 + core * line

    barrier = pltpu.get_barrier_semaphore()
    plane = [around(i) for i in range(1, ring)]
    beside = []
    for turn in ((pairs - 1, 1) if pairs > 1 else ()):
        for c in (0, 1):
            beside.append({"space": 2 * lax.rem(pair + turn, pairs) + c})
    greet(barrier, 1)
    expected = greetings(1) + len(beside)
    for peer in beside:
        pl.semaphore_signal(barrier, inc=1, device_id=peer, device_id_type=MESH)
    if pairs > 1:
        for edge, across in ((0, to_north), (ring - 1, to_south)):
            @pl.when(own == edge)
            def _():
                pl.semaphore_signal(barrier, inc=1, device_id=across, device_id_type=MESH)
        expected = expected + jnp.where((own == 0) | (own == ring - 1), 1, 0)

    quarter = columns // 4

    def column(place_of):
        return 4 * lax.rem(place_of, quarter) + 2 * lax.rem(lax.div(place_of, quarter), 2) + lax.div(place_of, 2 * quarter)

    pick[...] = jnp.where(iota((columns, columns), 0) == column(iota((1, columns), 1)), 1.0, 0.0).astype(BF16)
    loads[0].wait()
    loads[1].wait()
    both = jnp.concatenate([u_in[0].reshape(fields * half, columns), f_in[...].reshape(-1, columns)], axis=0)
    moved = exact_move(both, pick[...]).reshape(count // 2, half, columns)
    for k in range(tm):
        rows = moved[:, k * block : (k + 1) * block]
        two = jnp.stack([rows[..., :cols], rows[..., cols:]], axis=1)
        near[core * tm + k] = two.reshape(count * block, cols)

    pl.semaphore_wait(barrier, expected)
    mine = near.at[pl.ds(core * tm, tm)]
    swap = pltpu.make_async_remote_copy(mine, mine, near_send, near_recv,
                                        device_id={"space": 2 * pair + 1 - core}, device_id_type=MESH)
    swap.start()
    if pairs > 1:
        edge = near.at[pl.ds(core * (ring - 2), 2)]
        there = 2 * lax.rem(pair + pairs - 1 + 2 * core, pairs)
        far = [pltpu.make_async_remote_copy(edge, near.at[pl.ds(ring + 2 * core, 2)], far_send.at[c], far_recv.at[core],
                                            device_id={"space": there + c}, device_id_type=MESH) for c in (0, 1)]
        for c in far:
            c.start()
    greet(reach.at[0], 1)

    for c in loads[2:]:
        c.wait()
    place[...] = jnp.where(iota((columns, columns), 1) == column(iota((columns, 1), 0)), 1.0, 0.0).astype(BF16)
    for h in range(block // 2):
        q, k = iota((wide, 2 * groups), 1), iota((wide, 2 * groups), 0)
        fq, aq, bq = q // 4, (q // 2) % 2, q % 2
        gk, rk = k // block, k % block
        sel = jnp.where((gk == 2 * fq + bq) & (rk == 2 * h + aq), 1.0, 0.0).astype(BF16)
        wu4[:, h * ch : (h + 1) * ch] = jnp.dot(sel, wu_ref[...], preferred_element_type=F32).astype(BF16)
        wd4[h * ch : (h + 1) * ch] = jnp.dot(sel, wd_ref[...], preferred_element_type=F32).T.astype(BF16)
    for l in range(layers):
        w = wp_ref[l].astype(F32)
        for a in range(3):
            for b in range(3):
                tap = dk_ref[3 * a + b, l : l + 1, :]
                wcs[l, b * ch : (b + 1) * ch, a * ch : (a + 1) * ch] = (w * tap).astype(BF16)

    def down(pieces):
        x = jnp.concatenate([p.astype(BF16) for p in pieces], axis=1)
        return jnp.dot(wd4[...], x, preferred_element_type=F32).astype(BF16)

    def conv(l, a, x):
        y = jnp.dot(wcs[l, :, a * ch : a * ch + x.shape[0]], x, preferred_element_type=F32)
        lifted = []
        for c in range(0, x.shape[1], cols):
            lifted.append(y[ch : 2 * ch, c : c + cols] + from_west(y[:ch, c : c + cols])
                          + from_east(y[2 * ch :, c : c + cols]))
        return jnp.concatenate(lifted, axis=1)

    def mixed(old, lifted):
        return (old.astype(F32) + gelu(lifted)).astype(BF16)

    def blocks(hidden, first):
        for l in range(first, layers):
            new = []
            for r in range(hidden.shape[0] // ch - 2):
                new.append(mixed(hidden[(r + 1) * ch : (r + 2) * ch], conv(l, 0, hidden[r * ch : (r + 3) * ch])))
            hidden = jnp.concatenate(new, axis=0)
        deltas = []
        for r in range(0, hidden.shape[0], 2 * ch):
            deltas.append(jnp.dot(wu4[...], hidden[r : r + 2 * ch], preferred_element_type=F32))
        return [[d[:, c : c + cols] for d in deltas] for c in range(0, hidden.shape[1], cols)]

    def coarse(tasks):
        return blocks(jnp.concatenate([down(pieces) for pieces in zip(*tasks)], axis=0), 0)

    def coarse_own(own_pieces):
        h = down(own_pieces)
        return h, [conv(0, 2, h[:ch]), conv(0, 1, h), conv(0, 0, h), conv(0, 0, h[ch:])]

    def coarse_rest(begun, norths, souths):
        h, part = begun
        hn, hs = down(norths), down(souths)
        new = [
            mixed(hn[ch:], part[0] + conv(0, 0, hn)),
            mixed(h[:ch], part[1] + conv(0, 0, hn[ch:])),
            mixed(h[ch:], part[2] + conv(0, 2, hs[:ch])),
            mixed(hs[:ch], part[3] + conv(0, 1, hs)),
        ]
        return [d[0] for d in blocks(jnp.concatenate(new, axis=0), 1)]

    def in_rows(pieces):
        pieces = [p.astype(F32).reshape(-1, block, cols) for p in pieces]
        if len(pieces) * block % 8:
            pieces.append(jnp.zeros_like(pieces[0]))
        return jnp.concatenate(pieces, axis=1)

    def fine(pieces, force):
        done = fine_sweep(in_rows(pieces), force)
        return [done[:, (k + 1) * block : (k + 2) * block].reshape(wide, cols) for k in range(len(pieces) - 2)]

    def exchange(i, src, from_north, from_south):
        copies = [
            pltpu.make_async_remote_copy(src, from_south, send_sem.at[i, 0], recv_sem.at[i, 0],
                                         device_id=to_north, device_id_type=MESH),
            pltpu.make_async_remote_copy(src, from_north, send_sem.at[i, 1], recv_sem.at[i, 1],
                                         device_id=to_south, device_id_type=MESH),
        ]
        for c in copies:
            c.start()
        return copies

    row_place = lax.rem(own, tm)
    keeper = 2 * pair + lax.div(own, tm)

    others = (3 * (1 - lax.div(e, 2)), 2 - lax.div(e, 2), e + 1 - 2 * lax.rem(e, 2))

    def settle(n, end):
        x = end.astype(BF16).astype(F32).reshape(fields, 2, block, cols)
        flat = jnp.concatenate([x[:, 0].reshape(-1, cols), x[:, 1].reshape(-1, cols)], axis=1).astype(BF16)
        ebuf[n] = jnp.dot(flat, place[...], preferred_element_type=F32).astype(BF16)

    def ship(n):
        for k in range(1, ens):
            end_copy(n, k).start()
        here = (t == n) & (s == keeper)

        @pl.when(here)
        def _():
            pltpu.make_async_copy(ebuf.at[n], got.at[e, row_place], end_recv.at[e]).start()

        @pl.when(jnp.logical_not(here))
        def _():
            end_copy(n, 0).start()

    def end_copy(n, k):
        return pltpu.make_async_remote_copy(
            ebuf.at[n], got.at[e, row_place], end_send.at[n, k], end_recv.at[e],
            device_id={"tm": n, "space": keeper, "ens": others[k - 1] if k else e}, device_id_type=MESH)

    def sent(n):
        for k in range(1, ens):
            end_copy(n, k).wait_send()

        @pl.when((t != n) | (s != keeper))
        def _():
            end_copy(n, 0).wait_send()

    def collect():
        for n in range(tm):
            sent(n)
        total = []
        for member in (e,) + others[::-1]:
            pltpu.make_async_copy(got.at[member], got.at[member], end_recv.at[member]).wait()
            ends = [got[member, p].astype(F32) for p in range(tm)]
            if total:
                total = [x + y for x, y in zip(total, ends)]
            else:
                total = ends
                for p in range(tm):
                    both_ref[0, :, p * block : (p + 1) * block] = ends[p].reshape(fields, block, columns)
        for p in range(tm):
            both_ref[1, :, p * block : (p + 1) * block] = (total[p] * (1.0 / ens)).reshape(fields, block, columns)

    swap.wait()
    if pairs > 1:
        for c in (0, 1):
            far[c].wait_send()
            pltpu.make_async_copy(near.at[pl.ds(0, 2)], near.at[pl.ds(ring + 2 * c, 2)], far_recv.at[c]).wait()
    depth = near.shape[0]
    everything = [near[lax.rem(own + depth - 2 + k, depth)] for k in range(5)]
    start = [x[:wide] for x in everything]
    force = in_rows([x[wide:] for x in everything])
    force_near = in_rows([x[wide:] for x in everything[1:4]])

    v1 = fine(start, force)
    w2 = fine(v1, force_near)[0]
    u1 = [x + d for x, d in zip(start[1:4], coarse([start])[0])]
    snd_w[...] = w2.astype(BF16)
    moving_w = exchange(0, snd_w, nrt_w, sth_w)
    pl.semaphore_wait(reach.at[0], greetings(1))
    greet(reach.at[1], 2)

    fu1 = fine(u1, force_near)[0]
    du1, dv1 = coarse([u1, v1])
    u2 = u1[1] + du1[0]
    v2 = v1[1] + dv1[0] + (fu1 - u2)
    snd[0, 0] = u2.astype(BF16)
    snd[0, 1] = v2.astype(BF16)
    moving = exchange(1, snd.at[0], nrt.at[0], sth.at[0])
    pl.semaphore_wait(reach.at[1], greetings(2))
    for peer in plane:
        pl.semaphore_signal(reach.at[2], inc=1, device_id=peer, device_id_type=MESH)
    begun = coarse_own([u2, v2])
    for c in moving_w:
        c.wait()
    gw2 = w2 + coarse([[nrt_w[...], w2, sth_w[...]]])[0][0]
    pl.semaphore_wait(reach.at[2], len(plane))
    settle(0, v1[1])
    settle(1, w2)
    ship(0)
    ship(1)
    for c in moving:
        c.wait()
    fu2 = fine([nrt[0, 0], u2, sth[0, 0]], force_near)[0]
    fv2 = fine([nrt[0, 1], v2, sth[0, 1]], force_near)[0]
    du2, dv2 = coarse_rest(begun, [nrt[0, 0], nrt[0, 1]], [sth[0, 0], sth[0, 1]])
    gv2 = v2 + dv2
    v3 = gv2 + (fu2 - (u2 + du2))
    w3 = gw2 + (fv2 - gv2)
    snd[1, 0] = v3.astype(BF16)
    snd[1, 1] = w3.astype(BF16)
    moving = exchange(2, snd.at[1], nrt.at[1], sth.at[1])
    settle(2, w3)
    begun = coarse_own([v3, w3])
    for c in moving:
        c.wait()
    ship(2)
    fv3 = fine([nrt[1, 0], v3, sth[1, 0]], force_near)[0]
    dv3, dw3 = coarse_rest(begun, [nrt[1, 0], nrt[1, 1]], [sth[1, 0], sth[1, 1]])
    settle(3, w3 + dw3 + (fv3 - (v3 + dv3)))
    ship(3)
    collect()


def local(initial_state, forcing, w_down, depth_kernel, w_point, w_up):
    tm, spaces, ens = lax.axis_size("tm"), lax.axis_size("space"), lax.axis_size("ens")
    _, fields, half, columns = initial_state.shape
    block = half // tm
    cols, groups = columns // 2, 2 * fields
    layers, ch, _ = depth_kernel.shape
    assert block == FINE == 2 * layers == 4 and tm == 4
    assert spaces % 2 == 0 and ens == 4 and columns % 512 == 0
    count = groups + 2 * forcing.shape[0]
    near = 2 * tm + (4 if spaces > 2 else 0)
    vmem = pl.BlockSpec(memory_space=pltpu.VMEM)
    hbm = pl.BlockSpec(memory_space=pltpu.HBM)
    args = (initial_state, forcing, w_down.T, depth_kernel.transpose(2, 0, 1), w_point, w_up)
    args = tuple(pltpu.with_memory_space_constraint(a, pltpu.HBM) for a in args)
    both = pl.pallas_call(
        lambda *refs: kernel(tm, spaces, ens, *refs),
        name="parareal",
        out_shape=pltpu.VMEM((2, fields, half, columns), F32),
        in_specs=[hbm] * 6,
        out_specs=vmem,
        scratch_shapes=[pltpu.VMEM(a.shape, a.dtype) for a in args] + [
            pltpu.VMEM((columns, columns), BF16),
            pltpu.VMEM((columns, columns), BF16),
            pltpu.VMEM((2 * ch, groups * block), BF16),
            pltpu.VMEM((groups * block, 2 * ch), BF16),
            pltpu.VMEM((layers, 3 * ch, 3 * ch), BF16),
            pltpu.VMEM((near, count * block, cols), F32),
            pltpu.VMEM((groups * block, cols), BF16),
            pltpu.VMEM((groups * block, cols), BF16),
            pltpu.VMEM((groups * block, cols), BF16),
            pltpu.VMEM((2, 2, groups * block, cols), BF16),
            pltpu.VMEM((2, 2, groups * block, cols), BF16),
            pltpu.VMEM((2, 2, groups * block, cols), BF16),
            pltpu.VMEM((tm, fields * block, columns), BF16),
            pltpu.VMEM((ens, tm, fields * block, columns), BF16),
            pltpu.SemaphoreType.DMA((6,)),
            pltpu.SemaphoreType.DMA,
            pltpu.SemaphoreType.DMA,
            pltpu.SemaphoreType.DMA((2,)),
            pltpu.SemaphoreType.DMA((2,)),
            pltpu.SemaphoreType.DMA((3, 2)),
            pltpu.SemaphoreType.DMA((3, 2)),
            pltpu.SemaphoreType.DMA((tm, ens)),
            pltpu.SemaphoreType.DMA((ens,)),
            pltpu.SemaphoreType.REGULAR((3,)),
        ],
        compiler_params=pltpu.CompilerParams(has_side_effects=True, collective_id=0, vmem_limit_bytes=40 << 20),
    )(*args)
    return both[0][None, None], both[1][None]


def solution(mesh):
    in_specs = (P("ens", None, "space", None), P(None, "space", None), P(), P(), P(), P())
    out_specs = (P("ens", "tm", None, "space", None), P("tm", None, "space", None))
    return jax.shard_map(local, mesh=mesh, in_specs=in_specs, out_specs=out_specs, check_vma=False)
```
